32 devices in a mesh: hi: 4 (over x, core), lo: 8 (over z, y).
Axes of the slice: x: 2, y: 2, z: 4, core: 2. Of those that a mesh axis runs over, the one named last changes fastest.
Arguments:
- current: float32 [131072, 256], P(('hi', 'lo')), may hold values from -130 to 130
- signs: int32 [131072], P(('hi', 'lo')), may hold values from -1 to 1, as said below
- sample_rows: int32 [512], P(('hi', 'lo')), may hold values from 0 to 4095
- sample_owner: int32 [512, 1], P(('hi', 'lo')), may hold values from 0 to 7; in each aligned block of 16 rows (0 to 15, 16 to 31, ...) at most 2 rows name the same one
Outputs:
- sketch: float32 [4, 8, 8, 2, 256], P('hi', 'lo')
- r_factor: float32 [256, 256], replicated
- precond: float32 [131072, 256], P(('hi', 'lo'))
The draws below stay inside these ranges and needn't reach their ends.
Inputs may be any that keep to these rules, and one draw needn't show every extreme that they name: `signs`: each entry is -1 or 1. `sample_owner`: among the 16 samples of one device no owner is named more than 2 times, and in every draw some device names some owner exactly 2 times.
All inputs are finite; a program needn't handle non-finite values.
Results may differ from the reference program's by a relative error of at most 0.000098.
Values sent between devices are 32-bit elements; how exact they have to be, the bound alone decides.
A program may use at most 64 MiB of HBM per device.

```python
import math
import jax
import jax.numpy as jnp
import numpy as np
from jax import lax

P_SIZE = 256
ROWS_DEV = 4096
SAMP_DEV = 16
MOST = 2
TOTAL_ROWS = 131072
SAMPLES = 512
N_HI = 4
N_LO = 8


def draw_current(key, part):
    key_vals, key_rows, key_cols = jax.random.split(key, 3)
    row_scale = jnp.exp(jax.random.uniform(key_rows, (TOTAL_ROWS, 1), jnp.float32, -1.15, 1.15))
    col_scale = jnp.exp(jax.random.uniform(key_cols, (1, P_SIZE), jnp.float32, -1.15, 1.15))
    ramp_rows = 1.0 + 2.0 * jnp.arange(TOTAL_ROWS, dtype=jnp.float32)[:, None] / (TOTAL_ROWS - 1)
    values_base = jnp.clip(jax.random.normal(key_vals, (TOTAL_ROWS, P_SIZE), jnp.float32), -4.0, 4.0)
    return values_base * row_scale * ramp_rows * col_scale


def draw_signs(key, part):
    return (2 * jax.random.randint(key, (TOTAL_ROWS,), 0, 2) - 1).astype(jnp.int32)


def place_ends(drawn, stream_key, least, top_value):
    dims = drawn.shape
    spot = [jax.random.randint(jax.random.fold_in(stream_key, axis), (), 0, dims[axis]) for axis in range(len(dims))]
    drawn = drawn.at[tuple(spot)].set(least)
    longest = dims.index(max(dims))
    spot[longest] = (spot[longest] + 1) % dims[longest]
    return drawn.at[tuple(spot)].set(top_value)


def assign_block(stream_key, own, number, rows, count, top, bound, lean):
    sequence = jax.random.permutation(stream_key, count)
    packed, usual = shares(count, rows * top, bound, lean, True), shares(count, rows * top, bound, lean, False)
    places = jnp.arange(count)

    def named(tallies, turn):
        used = int((tallies > 0).sum())
        fixed = max(1, used // 4)
        shifted = fixed + (places - fixed + turn * (used - fixed)) % max(1, count - fixed)
        return jnp.zeros((count,), jnp.int32).at[sequence[jnp.where(places < fixed, places, shifted)]].set(jnp.asarray(tallies, jnp.int32))

    tallies = jnp.where(number % 4 == 0, named(packed, number // 4), named(usual, number - number // 4 - 1))
    mixed = jax.random.permutation(jax.random.fold_in(own, 3), count)
    giver, receiver = mixed[0:count // 2 * 2:2], mixed[1:count // 2 * 2:2]
    slack = jnp.minimum(tallies[giver] - 1, bound - tallies[receiver]) // 2
    slack = jnp.where((giver == sequence[0]) | (receiver == sequence[0]) | (tallies[receiver] == 0), 0, jnp.maximum(slack, 0))
    shifted = jax.random.randint(jax.random.fold_in(own, 4), (count // 2,), 0, 1 << 20) % (slack + 1)
    tallies = tallies.at[giver].add(-shifted).at[receiver].add(shifted)
    labels = jnp.searchsorted(jnp.cumsum(tallies), jnp.arange(rows * top), side="right").astype(jnp.int32)
    table = labels.reshape(top, rows).T
    table = table[jax.random.permutation(jax.random.fold_in(own, 1), rows)]
    turn = jax.random.randint(jax.random.fold_in(own, 2), (rows, 1), 0, top)
    return jnp.take_along_axis(table, (jnp.arange(top)[None, :] + turn) % top, axis=1)


def shares(count, total, most, slope, full):
    portions = [(1 << 20) // math.isqrt(rank ** slope) + 1 for rank in range(1, count + 1)]
    largest = most if full else min(most, max(-(-total // count), total * portions[0] // sum(portions)))
    least = 1 if total - largest >= count - 1 else 0
    holding, rest = [largest] + [least] * (count - 1), total - largest - least * (count - 1)
    while rest > 0:
        candidates = [i for i in range(1, count) if holding[i] < largest] or [i for i in range(1, count) if holding[i] < most]
        mass, left = sum([portions[i] for i in candidates]), rest
        for i in candidates:
            more = min(most - holding[i], max(1, left * portions[i] // mass), rest)
            holding[i] = holding[i] + more
            rest = rest - more
    return np.array(holding)


def setup_inputs(seed: int = 0) -> dict:
    keys = jax.random.split(jax.random.key(seed), 5)
    current = draw_current(jax.random.fold_in(keys[4], 71), 0)
    signs = draw_signs(jax.random.fold_in(keys[4], 71), 0)
    sample_rows = place_ends(jax.random.randint(keys[2], (SAMPLES,), 0, ROWS_DEV), jax.random.fold_in(keys[2], 1), 0, ROWS_DEV - 1).astype(jnp.int32)
    sample_owner_keys = jax.random.split(jax.random.fold_in(keys[3], 1), SAMPLES // SAMP_DEV)
    sample_owner_turns = jax.random.permutation(jax.random.fold_in(keys[3], 3), SAMPLES // SAMP_DEV)
    sample_owner = jax.vmap(lambda own, number: assign_block(jax.random.fold_in(keys[3], 2), own, number, SAMP_DEV, N_LO, 1, MOST, 2))(sample_owner_keys, sample_owner_turns).reshape((SAMPLES, 1))
    return dict(current=current, signs=signs, sample_rows=sample_rows, sample_owner=sample_owner)


HIGHEST = lax.Precision.HIGHEST

def sylvester(order_size):
    hadamard_table = jnp.ones((1, 1), jnp.float32)
    base_pair = jnp.array([[1.0, 1.0], [1.0, -1.0]], jnp.float32)
    while hadamard_table.shape[0] < order_size:
        hadamard_table = jnp.kron(hadamard_table, base_pair)
    return hadamard_table

def split_order(order_size):
    leading = 2 ** ((order_size.bit_length() - 1) // 2)
    return (leading, order_size // leading)

def reference(current, signs, sample_rows, sample_owner):
    devices = N_HI * N_LO
    signed = current * signs.astype(jnp.float32)[:, None]
    leading, second = split_order(ROWS_DEV)
    shaped = signed.reshape(devices, leading, second, P_SIZE)
    shaped = jnp.einsum('ab,gbcp->gacp', sylvester(leading), shaped, precision=HIGHEST)
    shaped = jnp.einsum('cd,gadp->gacp', sylvester(second), shaped, precision=HIGHEST)
    shaped = shaped.reshape(devices, ROWS_DEV, P_SIZE)
    crossed = jnp.einsum('gh,hrp->grp', sylvester(devices), shaped, precision=HIGHEST)
    flat_rows = crossed.reshape(TOTAL_ROWS, P_SIZE)
    device_of = jnp.arange(SAMPLES, dtype=jnp.int32) // SAMP_DEV
    global_rows = (device_of * ROWS_DEV + sample_rows).astype(jnp.int32)
    picked = jnp.take(flat_rows, global_rows, axis=0) * (1.0 / math.sqrt(TOTAL_ROWS))
    owner_ids = sample_owner[:, 0]
    owner_hot = (owner_ids[:, None] == jnp.arange(N_LO, dtype=jnp.int32)[None, :]).astype(jnp.int32)
    hot_device = owner_hot.reshape(devices, SAMP_DEV, N_LO)
    before = jnp.cumsum(hot_device, axis=1) - hot_device
    slot_ids = lax.optimization_barrier(jnp.sum(before * hot_device, axis=2)).reshape(SAMPLES)
    sketch = jnp.zeros((N_HI, N_LO, N_LO, MOST, P_SIZE), jnp.float32)
    sketch = sketch.at[device_of // N_LO, owner_ids, device_of % N_LO, slot_ids].set(picked)
    gram_total = jnp.dot(picked.T, picked, precision=HIGHEST) * (1.0 / SAMPLES)
    lower_factor = jnp.linalg.cholesky(gram_total)
    precond = lax.linalg.triangular_solve(lower_factor, current, left_side=False, lower=True, transpose_a=True)
    return (sketch, lower_factor.T, precond)
```

```python
import functools
import math

import jax
import jax.numpy as jnp
from jax import lax
from jax.experimental import pallas as pl
from jax.experimental.pallas import tpu as pltpu
from jax.sharding import PartitionSpec as P

MOST = 2
LANES = 128
BLOCK = 64
MESH = pl.DeviceIdType.MESH
HIGHEST = lax.Precision.HIGHEST
F32 = jnp.float32
BF16 = jnp.bfloat16


def bits_of(size):
    return size.bit_length() - 1


def reverse_bits(value, width):
    out = 0
    for bit in range(width):
        out |= ((value >> bit) & 1) << (width - 1 - bit)
    return out


def parity(value, top):
    shift = 1
    while shift * 2 < top:
        shift *= 2
    while shift >= 1:
        value = value ^ (value >> shift)
        shift //= 2
    return value & 1


def mix_kernel(nh, nl, count, note_ref, signs_ref, current_ref, gram_ref, sketch_ref,
               xbuf, xhi, xlo, notes, mat, share, landed, gathered,
               load_sem, nsend, nrecv, rsend, rrecv, gsend, grecv):
    hi, lo = lax.axis_index("hi"), lax.axis_index("lo")
    own = hi * nl + lo
    bh, bl = bits_of(nh), bits_of(nl)
    stages = bh + bl
    devices = nh * nl
    rows, width = current_ref.shape
    total = devices * count
    row_bits = bits_of(rows)
    loads = 8
    step = rows // loads

    def load(c):
        at = pl.ds(c * step, step)
        return pltpu.make_async_copy(current_ref.at[at, :], xbuf.at[at, :], load_sem.at[c])

    for c in range(loads):
        load(c).start()

    def peer(t):
        return (hi ^ (t >> bl), lo ^ (t & (nl - 1)))

    def place(t):
        return (reverse_bits(t >> bl, bh) << bl) | reverse_bits(t & (nl - 1), bl)

    barrier = pltpu.get_barrier_semaphore()
    for t in range(1, devices):
        pl.semaphore_signal(barrier, inc=1, device_id=peer(t), device_id_type=MESH)
    pl.semaphore_wait(barrier, devices - 1)

    def note(t):
        return pltpu.make_async_remote_copy(
            src_ref=note_ref, dst_ref=notes.at[pl.ds(place(t), 1), :],
            send_sem=nsend.at[t], recv_sem=nrecv.at[t],
            device_id=peer(t), device_id_type=MESH)

    for t in range(1, devices):
        note(t).start()
    notes[0:1, :] = note_ref[...]
    for c in range(loads):
        load(c).wait()

        @pl.loop(0, step // 64)
        def _(r):
            at = pl.ds(pl.multiple_of(c * step + r * 64, 64), 64)
            x = xbuf[at, :]
            top = x.astype(BF16)
            xhi[at, :] = top
            xlo[at, :] = (x - top.astype(F32)).astype(BF16)

    for t in range(1, devices):
        note(t).wait()

    chunk = min(256, total // 2)
    groups = chunk // count
    lane = lax.broadcasted_iota(jnp.int32, (chunk, LANES), 1)
    line = lax.broadcasted_iota(jnp.int32, (chunk, LANES), 0)

    def mix(first):
        part = notes[pl.ds(pl.multiple_of(first // count, groups), groups), :]
        wide = jnp.broadcast_to(part[:, None, :], (groups, count, LANES)).reshape(chunk, LANES)
        wide = jnp.where(lane == line % count, wide, 0.0)
        index = jnp.broadcast_to(jnp.sum(wide, axis=1, keepdims=True), (chunk, LANES))
        index = index.astype(jnp.int32)
        base = parity(index & (own * rows + lane), 2 ** (row_bits + stages).bit_length())
        base = (1 - 2 * base).astype(F32).astype(BF16)
        factors = []
        for bit in range(bits_of(rows // LANES)):
            flag = (index >> (bits_of(LANES) + bit)) & 1
            factors.append((1 - 2 * flag).astype(F32).astype(BF16))
        made = {0: base}
        for b in range(rows // LANES):
            if b:
                low = b & -b
                made[b] = made[b - low] * factors[bits_of(low)]
            sign = signs_ref[b:b + 1, :].astype(F32).astype(BF16)
            mat[:, b * LANES:(b + 1) * LANES] = made[b] * sign
        out = jnp.dot(mat[...], xhi[...], preferred_element_type=F32)
        out = out + jnp.dot(mat[...], xlo[...], preferred_element_type=F32)
        share[pl.ds(pl.multiple_of(first, chunk), chunk), :] = out

    def mix_range(first, last):
        if last - first == chunk:
            mix(first)
        else:
            @pl.loop(0, (last - first) // chunk)
            def _(k):
                mix(first + k * chunk)

    def stage_peer(s):
        return peer(1 << (bl + s)) if s < bh else peer(1 << (s - bh))

    def halve(s):
        half = total >> (s + 1)
        return pltpu.make_async_remote_copy(
            src_ref=share.at[pl.ds(half, half), :],
            dst_ref=landed.at[pl.ds(half, half), :],
            send_sem=rsend.at[s], recv_sem=rrecv.at[s],
            device_id=stage_peer(s), device_id_type=MESH)

    half = total // 2
    mix_range(half, total)
    halve(0).start()
    mix_range(0, half)
    for s in range(stages):
        half = total >> (s + 1)
        halve(s).wait_recv()
        if s < stages - 1:
            quarter = half // 2
            share[quarter:half, :] = share[quarter:half, :] + landed[half + quarter:half + half, :]
            halve(s + 1).start()
            share[0:quarter, :] = share[0:quarter, :] + landed[half:half + quarter, :]
        else:
            scale_all = 1.0 / math.sqrt(rows * devices)
            gathered[0:half, :] = (share[0:half, :] + landed[half:half + half, :]) * scale_all

    def double(s):
        size = total >> (s + 1)
        return pltpu.make_async_remote_copy(
            src_ref=gathered.at[pl.ds(0, size), :],
            dst_ref=gathered.at[pl.ds(size, size), :],
            send_sem=gsend.at[s], recv_sem=grecv.at[s],
            device_id=stage_peer(s), device_id_type=MESH)

    def product(first, size):
        block = gathered[first:first + size, :]
        return lax.dot_general(block, block, (((0,), (0,)), ((), ())),
                               precision=HIGHEST, preferred_element_type=F32)

    def sketch():
        span = nl * count
        owners = notes[0:nl, :]
        q = lax.broadcasted_iota(jnp.int32, (nl, LANES), 0)
        k = lax.broadcasted_iota(jnp.int32, (nl, LANES), 1)
        mine = (owners == lo.astype(F32)) & (k >= count) & (k < 2 * count)
        match = jnp.where(mine, 1.0, 0.0).astype(F32)
        up = lax.broadcasted_iota(jnp.int32, (LANES, LANES), 0)
        across = lax.broadcasted_iota(jnp.int32, (LANES, LANES), 1)
        ahead = jnp.where(up < across, 1.0, 0.0).astype(F32)
        before = jnp.dot(match, ahead, precision=HIGHEST, preferred_element_type=F32)
        spread_row = lax.broadcasted_iota(jnp.int32, (LANES, span), 0)
        spread_col = lax.broadcasted_iota(jnp.int32, (LANES, span), 1)
        spread = jnp.where(spread_row - count == spread_col % count, 1.0, 0.0).astype(F32)
        lead = lax.broadcasted_iota(jnp.int32, (nl, span), 0)
        cell = lax.broadcasted_iota(jnp.int32, (nl, span), 1)
        order_row = lax.broadcasted_iota(jnp.int32, (nl, nl), 0)
        order_col = lax.broadcasted_iota(jnp.int32, (nl, nl), 1)
        source = jnp.zeros((nl, nl), jnp.int32)
        for bit in range(bl):
            source = source | (((order_col >> bit) & 1) << (bl - 1 - bit))
        turn = jnp.where((source ^ lo) == order_row, 1.0, 0.0).astype(F32)
        rows_here = gathered[0:span, :]
        for m in range(MOST):
            chosen = jnp.where(jnp.abs(before - m) < 0.5, match, 0.0)
            wide = jnp.dot(chosen, spread, precision=HIGHEST, preferred_element_type=F32)
            wide = jnp.where(cell // count == lead, wide, 0.0)
            wide = jnp.dot(turn, wide, precision=HIGHEST, preferred_element_type=F32)
            sketch_ref[m, :, :] = jnp.dot(wide, rows_here, precision=HIGHEST,
                                          preferred_element_type=F32)

    for s in reversed(range(stages)):
        size = total >> (s + 1)
        double(s).start()
        if s == stages - 1:
            for r in range(stages):
                halve(r).wait_send()
        if s == bh - 1:
            sketch()
        if s == 0:
            gram_ref[...] = product(0, size)
        double(s).wait()
        if s == 0:
            gram_ref[...] = (gram_ref[...] + product(size, size)) * (1.0 / total)


def factor_kernel(gram_ref, sketch_in, current_ref, sketch_ref, r_ref, out_ref,
                  xbuf, obuf, load_sem, store_sem):
    rows, width = current_ref.shape
    pieces = 8
    step = rows // pieces

    def load(c):
        at = pl.ds(c * step, step)
        return pltpu.make_async_copy(current_ref.at[at, :], xbuf.at[at, :], load_sem.at[c])

    def store(c):
        at = pl.ds(c * step, step)
        return pltpu.make_async_copy(obuf.at[at, :], out_ref.at[at, :], store_sem.at[c])

    for c in range(pieces):
        load(c).start()
    for source in range(sketch_ref.shape[0]):
        for m in range(MOST):
            sketch_ref[source, m:m + 1, :] = sketch_in[m, source:source + 1, :]

    n = width
    blocks = n // BLOCK
    row = lax.broadcasted_iota(jnp.int32, (BLOCK, n), 0)
    col = lax.broadcasted_iota(jnp.int32, (BLOCK, n), 1)
    a = [gram_ref[k * BLOCK:(k + 1) * BLOCK, :] for k in range(blocks)]
    w = [jnp.where(row + k * BLOCK == col, 1.0, 0.0).astype(F32) for k in range(blocks)]
    sub = lax.broadcasted_iota(jnp.int32, (8, 2 * BLOCK), 0)
    small_row = lax.broadcasted_iota(jnp.int32, (BLOCK, BLOCK), 0)
    small_col = lax.broadcasted_iota(jnp.int32, (BLOCK, BLOCK), 1)
    unit = jnp.where(small_row == small_col, 1.0, 0.0).astype(F32)
    for k in range(blocks):
        at = slice(k * BLOCK, (k + 1) * BLOCK)
        both = jnp.concatenate([a[k][:, at], unit], axis=1)
        tiles = [both[8 * g:8 * g + 8, :] for g in range(BLOCK // 8)]
        for i in range(BLOCK - 1):
            g0, r0 = i // 8, i % 8
            pivot = tiles[g0][r0:r0 + 1, :]
            scaled = pivot / tiles[g0][r0:r0 + 1, i:i + 1]
            for g in range(g0, BLOCK // 8):
                if g == g0 and r0 == 7:
                    continue
                drop = tiles[g][:, i:i + 1] * scaled
                if g == g0:
                    drop = jnp.where(sub > r0, drop, 0.0)
                tiles[g] = tiles[g] - drop
        both = jnp.concatenate(tiles, axis=0)
        diag = jnp.sum(jnp.where(small_row == small_col, both[:, :BLOCK], 0.0), axis=1, keepdims=True)
        scale = 1.0 / jnp.sqrt(diag)
        inv = both[:, BLOCK:] * scale
        r_rows = jnp.dot(inv, a[k], precision=HIGHEST, preferred_element_type=F32)
        w_rows = jnp.dot(inv, w[k], precision=HIGHEST, preferred_element_type=F32)
        for later in range(k + 1, blocks):
            lower = lax.dot_general(a[later][:, at], inv, (((1,), (1,)), ((), ())),
                                    precision=HIGHEST, preferred_element_type=F32)
            a[later] = a[later] - jnp.dot(lower, r_rows, precision=HIGHEST, preferred_element_type=F32)
            w[later] = w[later] - jnp.dot(lower, w_rows, precision=HIGHEST, preferred_element_type=F32)
        r_ref[at, :] = jnp.where(row + k * BLOCK <= col, r_rows, 0.0)
        w[k] = w_rows
    inverse = jnp.concatenate(w, axis=0).T
    top = inverse.astype(BF16)
    rest = (inverse - top.astype(F32)).astype(BF16)
    for c in range(pieces):
        load(c).wait()
        at = slice(c * step, (c + 1) * step)
        x = xbuf[at, :]
        x_top = x.astype(BF16)
        x_rest = (x - x_top.astype(F32)).astype(BF16)
        y = jnp.dot(x_top, rest, preferred_element_type=F32)
        y = y + jnp.dot(x_rest, top, preferred_element_type=F32)
        y = y + jnp.dot(x_top, top, preferred_element_type=F32)
        obuf[at, :] = y
        store(c).start()
    for c in range(pieces):
        store(c).wait()


def shards(nh, nl, current, signs, sample_rows, sample_owner):
    rows, width = current.shape
    count = sample_rows.shape[0]
    devices = nh * nl
    total = devices * count
    stages = bits_of(devices)
    own = lax.axis_index("hi") * nl + lax.axis_index("lo")
    note = jnp.concatenate([own * rows + sample_rows, sample_owner[:, 0]])
    note = jnp.pad(note.astype(F32), (0, LANES - 2 * count))[None, :]
    vmem = pl.BlockSpec(memory_space=pltpu.VMEM)
    anywhere = pl.BlockSpec(memory_space=pl.ANY)
    dma = pltpu.SemaphoreType.DMA
    chunk = min(256, total // 2)
    gram, picked = pl.pallas_call(
        functools.partial(mix_kernel, nh, nl, count),
        name="mix",
        out_shape=(jax.ShapeDtypeStruct((width, width), F32),
                   jax.ShapeDtypeStruct((MOST, nl, width), F32)),
        in_specs=[vmem, vmem, anywhere],
        out_specs=(vmem, vmem),
        scratch_shapes=[
            pltpu.VMEM((rows, width), F32),
            pltpu.VMEM((rows, width), BF16),
            pltpu.VMEM((rows, width), BF16),
            pltpu.VMEM((devices, LANES), F32),
            pltpu.VMEM((chunk, rows), BF16),
            pltpu.VMEM((total, width), F32),
            pltpu.VMEM((total, width), F32),
            pltpu.VMEM((total, width), F32),
            dma((8,)), dma((devices,)), dma((devices,)),
            dma((stages,)), dma((stages,)), dma((stages,)), dma((stages,)),
        ],
        compiler_params=pltpu.CompilerParams(
            collective_id=0, has_side_effects=True, vmem_limit_bytes=48 * 2 ** 20),
    )(note, signs.reshape(rows // LANES, LANES), current)
    sketch, r_factor, precond = pl.pallas_call(
        factor_kernel,
        name="factor",
        out_shape=(jax.ShapeDtypeStruct((nl, MOST, width), F32),
                   jax.ShapeDtypeStruct((width, width), F32),
                   jax.ShapeDtypeStruct((rows, width), F32)),
        in_specs=[vmem, vmem, anywhere],
        out_specs=(vmem, vmem, anywhere),
        scratch_shapes=[
            pltpu.VMEM((rows, width), F32),
            pltpu.VMEM((rows, width), F32),
            dma((8,)), dma((8,)),
        ],
        compiler_params=pltpu.CompilerParams(vmem_limit_bytes=48 * 2 ** 20),
    )(gram, picked, current)
    return (sketch.reshape(1, 1, nl, MOST, width), r_factor, precond)


def solution(mesh):
    placed = (P(("hi", "lo"), None), P(("hi", "lo")), P(("hi", "lo")), P(("hi", "lo"), None))
    return jax.shard_map(
        functools.partial(shards, mesh.shape["hi"], mesh.shape["lo"]),
        mesh=mesh,
        in_specs=placed,
        out_specs=(P("hi", "lo", None, None, None), P(), P(("hi", "lo"), None)),
        check_vma=False,
    )
```

```python
import functools
import math

import jax
import jax.numpy as jnp
from jax import lax
from jax.experimental import pallas as pl
from jax.experimental.pallas import tpu as pltpu
from jax.sharding import PartitionSpec as P

MOST = 2
LANES = 128
BLOCK = 64
VMEM_LIMIT = 61 * 2 ** 20
MESH = pl.DeviceIdType.MESH
HIGHEST = lax.Precision.HIGHEST
F32 = jnp.float32
BF16 = jnp.bfloat16


def bits_of(size):
    return size.bit_length() - 1


def reverse_bits(value, width):
    out = 0
    for bit in range(width):
        out |= ((value >> bit) & 1) << (width - 1 - bit)
    return out


def parity(value, top):
    shift = 1
    while shift * 2 < top:
        shift *= 2
    while shift >= 1:
        value = value ^ (value >> shift)
        shift //= 2
    return value & 1


def mix_kernel(nh, nl, count, rows_ref, owner_ref, signs_ref, current_ref, gram_ref, sketch_ref,
               note_ref, xbuf, xhi, xlo, notes, mat, share, landed, shared, gathered,
               load_sem, nsend, nrecv, rsend, rrecv, lsend, lrecv, asend, arecv, gsend, grecv):
    hi, lo = lax.axis_index("hi"), lax.axis_index("lo")
    own = hi * nl + lo
    bh, bl = bits_of(nh), bits_of(nl)
    stages = bh + bl
    devices = nh * nl
    rows, width = current_ref.shape
    total = devices * count
    row_bits = bits_of(rows)
    loads = 8
    step = rows // loads

    def load(c):
        at = pl.ds(c * step, step)
        return pltpu.make_async_copy(current_ref.at[at, :], xbuf.at[at, :], load_sem.at[c])

    for c in range(loads):
        load(c).start()

    tags = lax.broadcasted_iota(jnp.int32, (count, LANES), 1)
    spots = lax.broadcasted_iota(jnp.int32, (count, LANES), 0)
    named = jnp.broadcast_to(owner_ref[...].astype(F32), (count, LANES))
    named = jnp.where(tags == spots + count, named, 0.0)
    note_ref[...] = jnp.sum(named, axis=0, keepdims=True)
    note_ref[:, 0:count] = (rows_ref[...] + own * rows).astype(F32)

    def peer(t):
        return (hi ^ (t >> bl), lo ^ (t & (nl - 1)))

    def place(t):
        return (reverse_bits(t >> bl, bh) << bl) | reverse_bits(t & (nl - 1), bl)

    barrier = pltpu.get_barrier_semaphore()
    for t in range(1, devices):
        pl.semaphore_signal(barrier, inc=1, device_id=peer(t), device_id_type=MESH)
    pl.semaphore_wait(barrier, devices - 1)

    def note(t):
        return pltpu.make_async_remote_copy(
            src_ref=note_ref, dst_ref=notes.at[pl.ds(place(t), 1), :],
            send_sem=nsend.at[t], recv_sem=nrecv.at[t],
            device_id=peer(t), device_id_type=MESH)

    for t in range(1, devices):
        note(t).start()
    notes[0:1, :] = note_ref[...]
    for c in range(loads):
        load(c).wait()

        @pl.loop(0, step // 64)
        def _(r):
            at = pl.ds(pl.multiple_of(c * step + r * 64, 64), 64)
            x = xbuf[at, :]
            top = x.astype(BF16)
            xhi[at, :] = top
            xlo[at, :] = (x - top.astype(F32)).astype(BF16)

    for t in range(1, devices):
        note(t).wait()

    chunk = min(256, total // 2)
    groups = chunk // count
    lane = lax.broadcasted_iota(jnp.int32, (chunk, LANES), 1)
    line = lax.broadcasted_iota(jnp.int32, (chunk, LANES), 0)

    def mix(first):
        part = notes[pl.ds(pl.multiple_of(first // count, groups), groups), :]
        wide = jnp.broadcast_to(part[:, None, :], (groups, count, LANES)).reshape(chunk, LANES)
        wide = jnp.where(lane == line % count, wide, 0.0)
        index = jnp.broadcast_to(jnp.sum(wide, axis=1, keepdims=True), (chunk, LANES))
        index = index.astype(jnp.int32)
        base = parity(index & (own * rows + lane), 2 ** (row_bits + stages).bit_length())
        base = (1 - 2 * base).astype(F32).astype(BF16)
        factors = []
        for bit in range(bits_of(rows // LANES)):
            flag = (index >> (bits_of(LANES) + bit)) & 1
            factors.append((1 - 2 * flag).astype(F32).astype(BF16))
        made = {0: base}
        for b in range(rows // LANES):
            if b:
                low = b & -b
                made[b] = made[b - low] * factors[bits_of(low)]
            sign = signs_ref[b:b + 1, :].astype(F32).astype(BF16)
            mat[:, b * LANES:(b + 1) * LANES] = made[b] * sign
        out = jnp.dot(mat[...], xhi[...], preferred_element_type=F32)
        out = out + jnp.dot(mat[...], xlo[...], preferred_element_type=F32)
        share[pl.ds(pl.multiple_of(first, chunk), chunk), :] = out

    def mix_range(first, last):
        if last - first == chunk:
            mix(first)
        else:
            @pl.loop(0, (last - first) // chunk)
            def _(k):
                mix(first + k * chunk)

    def stage_peer(s):
        return peer(1 << (bl + s)) if s < bh else peer(1 << (s - bh))

    def halve(s):
        half = total >> (s + 1)
        return pltpu.make_async_remote_copy(
            src_ref=share.at[pl.ds(half, half), :],
            dst_ref=landed.at[pl.ds(half, half), :],
            send_sem=rsend.at[s], recv_sem=rrecv.at[s],
            device_id=stage_peer(s), device_id_type=MESH)

    span = nl * count
    half = total // 2
    mix_range(half, total)
    halve(0).start()
    mix_range(0, half)
    for s in range(bh):
        half = total >> (s + 1)
        quarter = half // 2
        halve(s).wait_recv()
        share[quarter:half, :] = share[quarter:half, :] + landed[half + quarter:half + half, :]
        if s < bh - 1:
            halve(s + 1).start()
        share[0:quarter, :] = share[0:quarter, :] + landed[half:half + quarter, :]

    def low_sum(t):
        return pltpu.make_async_remote_copy(
            src_ref=share.at[pl.ds(place(t) * count, count), :],
            dst_ref=shared.at[t],
            send_sem=lsend.at[t], recv_sem=lrecv.at[t],
            device_id=peer(t), device_id_type=MESH)

    def low_gather(t):
        return pltpu.make_async_remote_copy(
            src_ref=gathered.at[pl.ds(0, count), :],
            dst_ref=gathered.at[pl.ds(place(t) * count, count), :],
            send_sem=asend.at[t], recv_sem=arecv.at[t],
            device_id=peer(t), device_id_type=MESH)

    for t in reversed(range(1, nl)):
        low_sum(t).start()
    kept = share[0:count, :]
    for t in range(1, nl):
        low_sum(t).wait_recv()
        kept = kept + shared[t]
    gathered[0:count, :] = kept * (1.0 / math.sqrt(rows * devices))
    for t in reversed(range(1, nl)):
        low_gather(t).start()
    for t in range(1, nl):
        low_sum(t).wait_send()
    for r in range(bh):
        halve(r).wait_send()

    def pass_on(q, s):
        return pltpu.make_async_remote_copy(
            src_ref=gathered.at[pl.ds(q * span, span), :],
            dst_ref=gathered.at[pl.ds((q + (nh >> (s + 1))) * span, span), :],
            send_sem=gsend.at[s * nh + q], recv_sem=grecv.at[s * nh + q],
            device_id=stage_peer(s), device_id_type=MESH)

    def came_by(q):
        return bh - q.bit_length()

    def product(first, size):
        block = gathered[first:first + size, :]
        return lax.dot_general(block, block, (((0,), (0,)), ((), ())),
                               precision=HIGHEST, preferred_element_type=F32)

    def sketch():
        span = nl * count
        owners = notes[0:nl, :]
        q = lax.broadcasted_iota(jnp.int32, (nl, LANES), 0)
        k = lax.broadcasted_iota(jnp.int32, (nl, LANES), 1)
        mine = (owners == lo.astype(F32)) & (k >= count) & (k < 2 * count)
        match = jnp.where(mine, 1.0, 0.0).astype(F32)
        up = lax.broadcasted_iota(jnp.int32, (LANES, LANES), 0)
        across = lax.broadcasted_iota(jnp.int32, (LANES, LANES), 1)
        ahead = jnp.where(up < across, 1.0, 0.0).astype(F32)
        before = jnp.dot(match, ahead, precision=HIGHEST, preferred_element_type=F32)
        spread_row = lax.broadcasted_iota(jnp.int32, (LANES, span), 0)
        spread_col = lax.broadcasted_iota(jnp.int32, (LANES, span), 1)
        spread = jnp.where(spread_row - count == spread_col % count, 1.0, 0.0).astype(F32)
        lead = lax.broadcasted_iota(jnp.int32, (nl, span), 0)
        cell = lax.broadcasted_iota(jnp.int32, (nl, span), 1)
        order_row = lax.broadcasted_iota(jnp.int32, (nl, nl), 0)
        order_col = lax.broadcasted_iota(jnp.int32, (nl, nl), 1)
        source = jnp.zeros((nl, nl), jnp.int32)
        for bit in range(bl):
            source = source | (((order_col >> bit) & 1) << (bl - 1 - bit))
        turn = jnp.where((source ^ lo) == order_row, 1.0, 0.0).astype(F32)
        rows_here = gathered[0:span, :]
        for m in range(MOST):
            chosen = jnp.where(jnp.abs(before - m) < 0.5, match, 0.0)
            wide = jnp.dot(chosen, spread, precision=HIGHEST, preferred_element_type=F32)
            wide = jnp.where(cell // count == lead, wide, 0.0)
            wide = jnp.dot(turn, wide, precision=HIGHEST, preferred_element_type=F32)
            sketch_ref[m, :, :] = jnp.dot(wide, rows_here, precision=HIGHEST,
                                          preferred_element_type=F32)

    for t in range(1, nl):
        low_gather(t).wait_recv()
    for q in range(nh):
        if q:
            stage = came_by(q)
            pass_on(q - (nh >> (stage + 1)), stage).wait_recv()
        for s in reversed(range(came_by(q))):
            pass_on(q, s).start()
        if q == 0:
            sketch()
            gram_ref[...] = product(0, span)
        elif q < nh - 1:
            gram_ref[...] = gram_ref[...] + product(q * span, span)
        else:
            gram_ref[...] = (gram_ref[...] + product(q * span, span)) * (1.0 / total)
    for t in range(1, nl):
        low_gather(t).wait_send()
    for q in range(nh):
        for s in range(came_by(q)):
            pass_on(q, s).wait_send()


def eliminate(both, hook):
    nb = both.shape[0]
    sub = lax.broadcasted_iota(jnp.int32, (8, both.shape[1]), 0)
    wide = (8, both.shape[1])
    tiles = [both[8 * g:8 * g + 8, :] for g in range(nb // 8)]
    for g0 in range(nb // 8):
        hook()
        cols = {}
        for g in range(g0, nb // 8):
            cols[g] = [jnp.broadcast_to(tiles[g][:, 8 * g0 + j:8 * g0 + j + 1], wide) for j in range(8)]
        for i in range(8):
            if i == 7 and g0 == nb // 8 - 1:
                break
            lead = cols[g0]
            flip = 1.0 / lead[i][i:i + 1, :]
            pivot = tiles[g0][i:i + 1, :]
            heads = [lead[j][i:i + 1, :] for j in range(8)]
            for g in range(g0, nb // 8):
                if g == g0 and i == 7:
                    continue
                rate = cols[g][i] * flip
                if g == g0:
                    rate = jnp.where(sub > i, rate, 0.0)
                for j in range(i + 1, 8):
                    cols[g][j] = cols[g][j] - rate * heads[j]
                tiles[g] = tiles[g] - rate * pivot
    return jnp.concatenate(tiles, axis=0)


def factor_kernel(gram_ref, sketch_in, current_ref, sketch_ref, r_ref, out_ref,
                  xbuf, parts, obuf, load_sem, store_sem):
    rows, width = current_ref.shape
    pieces = 8
    step = rows // pieces

    def load(c):
        at = pl.ds(c * step, step)
        return pltpu.make_async_copy(current_ref.at[at, :], xbuf.at[at, :], load_sem.at[c])

    def store(c):
        at = pl.ds(c * step, step)
        return pltpu.make_async_copy(obuf.at[at, :], out_ref.at[at, :], store_sem.at[c])

    for c in range(pieces):
        load(c).start()
    for source in range(sketch_ref.shape[0]):
        for m in range(MOST):
            sketch_ref[source, m:m + 1, :] = sketch_in[m, source:source + 1, :]

    n = width
    blocks = n // BLOCK
    hooks = blocks * (BLOCK // 8)
    slab = rows // (hooks - BLOCK // 8)
    state = {"next": 0, "turn": 0}

    def split():
        state["turn"] += 1
        if state["turn"] <= BLOCK // 8 or state["next"] >= rows:
            return
        first = state["next"]
        last = min(rows, first + -(-slab // 16) * 16)
        state["next"] = last
        x = xbuf[first:last, :]
        top = x.astype(BF16)
        parts[first:last, 0:width] = top
        parts[first:last, width:2 * width] = (x - top.astype(F32)).astype(BF16)

    row = lax.broadcasted_iota(jnp.int32, (BLOCK, n), 0)
    col = lax.broadcasted_iota(jnp.int32, (BLOCK, n), 1)
    a = [gram_ref[k * BLOCK:(k + 1) * BLOCK, :] for k in range(blocks)]
    w = [jnp.where(row + k * BLOCK == col, 1.0, 0.0).astype(F32) for k in range(blocks)]
    small_row = lax.broadcasted_iota(jnp.int32, (BLOCK, BLOCK), 0)
    small_col = lax.broadcasted_iota(jnp.int32, (BLOCK, BLOCK), 1)
    unit = jnp.where(small_row == small_col, 1.0, 0.0).astype(F32)
    for k in range(blocks):
        at = slice(k * BLOCK, (k + 1) * BLOCK)
        if k == 1:
            for c in range(pieces):
                load(c).wait()
        both = eliminate(jnp.concatenate([a[k][:, at], unit], axis=1), split)
        diag = jnp.sum(jnp.where(small_row == small_col, both[:, :BLOCK], 0.0), axis=1, keepdims=True)
        scale = 1.0 / jnp.sqrt(diag)
        inv = both[:, BLOCK:] * scale
        r_rows = jnp.dot(inv, a[k], precision=HIGHEST, preferred_element_type=F32)
        w_rows = jnp.dot(inv, w[k], precision=HIGHEST, preferred_element_type=F32)
        for later in range(k + 1, blocks):
            lower = lax.dot_general(a[later][:, at], inv, (((1,), (1,)), ((), ())),
                                    precision=HIGHEST, preferred_element_type=F32)
            a[later] = a[later] - jnp.dot(lower, r_rows, precision=HIGHEST, preferred_element_type=F32)
            w[later] = w[later] - jnp.dot(lower, w_rows, precision=HIGHEST, preferred_element_type=F32)
        r_ref[at, :] = jnp.where(row + k * BLOCK <= col, r_rows, 0.0)
        w[k] = w_rows
    inverse = jnp.concatenate(w, axis=0).T
    top = inverse.astype(BF16)
    rest = (inverse - top.astype(F32)).astype(BF16)
    stack = jnp.concatenate([top, top, rest], axis=0)
    for c in range(pieces):
        at = slice(c * step, (c + 1) * step)
        x = parts[at, :]
        x = jnp.concatenate([x, x[:, 0:width]], axis=1)
        obuf[at, :] = jnp.dot(x, stack, preferred_element_type=F32)
        store(c).start()
    for c in range(pieces):
        store(c).wait()


def shards(nh, nl, current, signs, sample_rows, sample_owner):
    rows, width = current.shape
    count = sample_rows.shape[0]
    devices = nh * nl
    total = devices * count
    stages = bits_of(devices)
    vmem = pl.BlockSpec(memory_space=pltpu.VMEM)
    anywhere = pl.BlockSpec(memory_space=pl.ANY)
    dma = pltpu.SemaphoreType.DMA
    chunk = min(256, total // 2)
    gram, picked = pl.pallas_call(
        functools.partial(mix_kernel, nh, nl, count),
        name="mix",
        out_shape=(jax.ShapeDtypeStruct((width, width), F32),
                   jax.ShapeDtypeStruct((MOST, nl, width), F32)),
        in_specs=[vmem, vmem, vmem, anywhere],
        out_specs=(vmem, vmem),
        scratch_shapes=[
            pltpu.VMEM((1, LANES), F32),
            pltpu.VMEM((rows, width), F32),
            pltpu.VMEM((rows, width), BF16),
            pltpu.VMEM((rows, width), BF16),
            pltpu.VMEM((devices, LANES), F32),
            pltpu.VMEM((chunk, rows), BF16),
            pltpu.VMEM((total, width), F32),
            pltpu.VMEM((total, width), F32),
            pltpu.VMEM((nl, count, width), F32),
            pltpu.VMEM((total, width), F32),
            dma((8,)), dma((devices,)), dma((devices,)),
            dma((stages,)), dma((stages,)), dma((nl,)), dma((nl,)), dma((nl,)), dma((nl,)),
            dma((stages * nh,)), dma((stages * nh,)),
        ],
        compiler_params=pltpu.CompilerParams(
            collective_id=0, has_side_effects=True, vmem_limit_bytes=VMEM_LIMIT),
    )(sample_rows.reshape(1, count), sample_owner, signs.reshape(rows // LANES, LANES), current)
    sketch, r_factor, precond = pl.pallas_call(
        factor_kernel,
        name="factor",
        out_shape=(jax.ShapeDtypeStruct((nl, MOST, width), F32),
                   jax.ShapeDtypeStruct((width, width), F32),
                   jax.ShapeDtypeStruct((rows, width), F32)),
        in_specs=[vmem, vmem, anywhere],
        out_specs=(vmem, vmem, anywhere),
        scratch_shapes=[
            pltpu.VMEM((rows, width), F32),
            pltpu.VMEM((rows, 2 * width), BF16),
            pltpu.VMEM((rows, width), F32),
            dma((8,)), dma((8,)),
        ],
        compiler_params=pltpu.CompilerParams(vmem_limit_bytes=VMEM_LIMIT),
    )(gram, picked, current)
    return (sketch.reshape(1, 1, nl, MOST, width), r_factor, precond)


def solution(mesh):
    placed = (P(("hi", "lo"), None), P(("hi", "lo")), P(("hi", "lo")), P(("hi", "lo"), None))
    return jax.shard_map(
        functools.partial(shards, mesh.shape["hi"], mesh.shape["lo"]),
        mesh=mesh,
        in_specs=placed,
        out_specs=(P("hi", "lo", None, None, None), P(), P(("hi", "lo"), None)),
        check_vma=False,
    )
```

```python
import functools
import math

import jax
import jax.numpy as jnp
from jax import lax
from jax.experimental import pallas as pl
from jax.experimental.pallas import tpu as pltpu
from jax.sharding import PartitionSpec as P

MOST = 2
LANES = 128
BLOCK = 64
VMEM_LIMIT = 61 * 2 ** 20
MESH = pl.DeviceIdType.MESH
HIGHEST = lax.Precision.HIGHEST
F32 = jnp.float32
BF16 = jnp.bfloat16


def bits_of(size):
    return size.bit_length() - 1


def reverse_bits(value, width):
    out = 0
    for bit in range(width):
        out |= ((value >> bit) & 1) << (width - 1 - bit)
    return out


def parity(value, top):
    shift = 1
    while shift * 2 < top:
        shift *= 2
    while shift >= 1:
        value = value ^ (value >> shift)
        shift //= 2
    return value & 1


def mix_kernel(nh, nl, count, rows_hbm, owner_hbm, signs_hbm, current_ref, gram_ref, sketch_ref,
               rows_ref, owner_ref, signs_ref, note_ref, xbuf, xhi, xlo, notes, mat, share, landed, shared, gathered,
               small_sem, load_sem, nsend, nrecv, rsend, rrecv, lsend, lrecv, asend, arecv, gsend, grecv):
    hi, lo = lax.axis_index("hi"), lax.axis_index("lo")
    own = hi * nl + lo
    bh, bl = bits_of(nh), bits_of(nl)
    stages = bh + bl
    devices = nh * nl
    rows, width = current_ref.shape
    total = devices * count
    row_bits = bits_of(rows)
    loads = 8
    step = rows // loads

    def load(c):
        at = pl.ds(c * step, step)
        return pltpu.make_async_copy(current_ref.at[at, :], xbuf.at[at, :], load_sem.at[c])

    small = [pltpu.make_async_copy(source, target, small_sem.at[k])
             for k, (source, target) in enumerate(
                 ((rows_hbm, rows_ref), (owner_hbm, owner_ref), (signs_hbm, signs_ref)))]
    for copy in small:
        copy.start()

    def peer(t):
        return (hi ^ (t >> bl), lo ^ (t & (nl - 1)))

    def place(t):
        return (reverse_bits(t >> bl, bh) << bl) | reverse_bits(t & (nl - 1), bl)

    barrier = pltpu.get_barrier_semaphore()
    for t in range(1, devices):
        pl.semaphore_signal(barrier, inc=1, device_id=peer(t), device_id_type=MESH)
    for c in range(loads):
        load(c).start()
    for copy in small:
        copy.wait()
    note_ref[...] = jnp.zeros_like(note_ref)
    note_ref[:, 0:count] = (rows_ref[...] + own * rows).astype(F32)
    note_ref[:, count:2 * count] = owner_ref[...].astype(F32)
    pl.semaphore_wait(barrier, devices - 1)

    def note(t):
        return pltpu.make_async_remote_copy(
            src_ref=note_ref, dst_ref=notes.at[pl.ds(place(t), 1), :],
            send_sem=nsend.at[t], recv_sem=nrecv.at[t],
            device_id=peer(t), device_id_type=MESH)

    for t in range(1, devices):
        note(t).start()
    notes[0:1, :] = note_ref[...]
    for c in range(loads):
        load(c).wait()

        @pl.loop(0, step // 64)
        def _(r):
            at = pl.ds(pl.multiple_of(c * step + r * 64, 64), 64)
            x = xbuf[at, :]
            top = x.astype(BF16)
            xhi[at, :] = top
            xlo[at, :] = (x - top.astype(F32)).astype(BF16)

    for t in range(1, devices):
        note(t).wait()

    chunk = min(256, total // 2)
    groups = chunk // count
    lane = lax.broadcasted_iota(jnp.int32, (chunk, LANES), 1)
    line = lax.broadcasted_iota(jnp.int32, (chunk, LANES), 0)

    def mix(first):
        part = notes[pl.ds(pl.multiple_of(first // count, groups), groups), :]
        wide = jnp.broadcast_to(part[:, None, :], (groups, count, LANES)).reshape(chunk, LANES)
        wide = jnp.where(lane == line % count, wide, 0.0)
        index = jnp.broadcast_to(jnp.sum(wide, axis=1, keepdims=True), (chunk, LANES))
        index = index.astype(jnp.int32)
        base = parity(index & (own * rows + lane), 2 ** (row_bits + stages).bit_length())
        base = (1 - 2 * base).astype(F32).astype(BF16)
        factors = []
        for bit in range(bits_of(rows // LANES)):
            flag = (index >> (bits_of(LANES) + bit)) & 1
            factors.append((1 - 2 * flag).astype(F32).astype(BF16))
        made = {0: base}
        for b in range(rows // LANES):
            if b:
                low = b & -b
                made[b] = made[b - low] * factors[bits_of(low)]
            sign = signs_ref[b:b + 1, :].astype(F32).astype(BF16)
            mat[:, b * LANES:(b + 1) * LANES] = made[b] * sign
        out = jnp.dot(mat[...], xhi[...], preferred_element_type=F32)
        out = out + jnp.dot(mat[...], xlo[...], preferred_element_type=F32)
        share[pl.ds(pl.multiple_of(first, chunk), chunk), :] = out

    def mix_range(first, last):
        if last - first == chunk:
            mix(first)
        else:
            @pl.loop(0, (last - first) // chunk)
            def _(k):
                mix(first + k * chunk)

    def stage_peer(s):
        return peer(1 << (bl + s)) if s < bh else peer(1 << (s - bh))

    def halve(s):
        half = total >> (s + 1)
        return pltpu.make_async_remote_copy(
            src_ref=share.at[pl.ds(half, half), :],
            dst_ref=landed.at[pl.ds(half, half), :],
            send_sem=rsend.at[s], recv_sem=rrecv.at[s],
            device_id=stage_peer(s), device_id_type=MESH)

    span = nl * count
    half = total // 2
    mix_range(half, total)
    halve(0).start()
    mix_range(0, half)
    for s in range(bh):
        half = total >> (s + 1)
        quarter = half // 2
        halve(s).wait_recv()
        share[quarter:half, :] = share[quarter:half, :] + landed[half + quarter:half + half, :]
        if s < bh - 1:
            halve(s + 1).start()
        share[0:quarter, :] = share[0:quarter, :] + landed[half:half + quarter, :]

    def low_sum(t):
        return pltpu.make_async_remote_copy(
            src_ref=share.at[pl.ds(place(t) * count, count), :],
            dst_ref=shared.at[t],
            send_sem=lsend.at[t], recv_sem=lrecv.at[t],
            device_id=peer(t), device_id_type=MESH)

    def low_gather(t):
        return pltpu.make_async_remote_copy(
            src_ref=gathered.at[pl.ds(0, count), :],
            dst_ref=gathered.at[pl.ds(place(t) * count, count), :],
            send_sem=asend.at[t], recv_sem=arecv.at[t],
            device_id=peer(t), device_id_type=MESH)

    for t in reversed(range(1, nl)):
        low_sum(t).start()
    kept = share[0:count, :]
    for t in range(1, nl):
        low_sum(t).wait_recv()
        kept = kept + shared[t]
    gathered[0:count, :] = kept * (1.0 / math.sqrt(rows * devices))
    for t in reversed(range(1, nl)):
        low_gather(t).start()
    for t in range(1, nl):
        low_sum(t).wait_send()
    for r in range(bh):
        halve(r).wait_send()

    def pass_on(q, s):
        return pltpu.make_async_remote_copy(
            src_ref=gathered.at[pl.ds(q * span, span), :],
            dst_ref=gathered.at[pl.ds((q + (nh >> (s + 1))) * span, span), :],
            send_sem=gsend.at[s * nh + q], recv_sem=grecv.at[s * nh + q],
            device_id=stage_peer(s), device_id_type=MESH)

    def came_by(q):
        return bh - q.bit_length()

    def product(first, size):
        block = gathered[first:first + size, :]
        return lax.dot_general(block, block, (((0,), (0,)), ((), ())),
                               precision=HIGHEST, preferred_element_type=F32)

    def sketch():
        span = nl * count
        owners = notes[0:nl, :]
        q = lax.broadcasted_iota(jnp.int32, (nl, LANES), 0)
        k = lax.broadcasted_iota(jnp.int32, (nl, LANES), 1)
        mine = (owners == lo.astype(F32)) & (k >= count) & (k < 2 * count)
        match = jnp.where(mine, 1.0, 0.0).astype(F32)
        up = lax.broadcasted_iota(jnp.int32, (LANES, LANES), 0)
        across = lax.broadcasted_iota(jnp.int32, (LANES, LANES), 1)
        ahead = jnp.where(up < across, 1.0, 0.0).astype(F32)
        before = jnp.dot(match, ahead, precision=HIGHEST, preferred_element_type=F32)
        spread_row = lax.broadcasted_iota(jnp.int32, (LANES, span), 0)
        spread_col = lax.broadcasted_iota(jnp.int32, (LANES, span), 1)
        spread = jnp.where(spread_row - count == spread_col % count, 1.0, 0.0).astype(F32)
        lead = lax.broadcasted_iota(jnp.int32, (nl, span), 0)
        cell = lax.broadcasted_iota(jnp.int32, (nl, span), 1)
        order_row = lax.broadcasted_iota(jnp.int32, (nl, nl), 0)
        order_col = lax.broadcasted_iota(jnp.int32, (nl, nl), 1)
        source = jnp.zeros((nl, nl), jnp.int32)
        for bit in range(bl):
            source = source | (((order_col >> bit) & 1) << (bl - 1 - bit))
        turn = jnp.where((source ^ lo) == order_row, 1.0, 0.0).astype(F32)
        rows_here = gathered[0:span, :]
        for m in range(MOST):
            chosen = jnp.where(jnp.abs(before - m) < 0.5, match, 0.0)
            wide = jnp.dot(chosen, spread, precision=HIGHEST, preferred_element_type=F32)
            wide = jnp.where(cell // count == lead, wide, 0.0)
            wide = jnp.dot(turn, wide, precision=HIGHEST, preferred_element_type=F32)
            sketch_ref[m, :, :] = jnp.dot(wide, rows_here, precision=HIGHEST,
                                          preferred_element_type=F32)

    for t in range(1, nl):
        low_gather(t).wait_recv()
    for q in range(nh):
        if q:
            stage = came_by(q)
            pass_on(q - (nh >> (stage + 1)), stage).wait_recv()
        for s in reversed(range(came_by(q))):
            pass_on(q, s).start()
        if q == 0:
            sketch()
            gram_ref[...] = product(0, span)
        elif q < nh - 1:
            gram_ref[...] = gram_ref[...] + product(q * span, span)
        else:
            gram_ref[...] = (gram_ref[...] + product(q * span, span)) * (1.0 / total)
    for t in range(1, nl):
        low_gather(t).wait_send()
    for q in range(nh):
        for s in range(came_by(q)):
            pass_on(q, s).wait_send()


def eliminate(both, hook):
    nb = both.shape[0]
    sub = lax.broadcasted_iota(jnp.int32, (8, both.shape[1]), 0)
    wide = (8, both.shape[1])
    tiles = [both[8 * g:8 * g + 8, :] for g in range(nb // 8)]
    for g0 in range(nb // 8):
        hook()
        cols = {}
        for g in range(g0, nb // 8):
            cols[g] = [jnp.broadcast_to(tiles[g][:, 8 * g0 + j:8 * g0 + j + 1], wide) for j in range(8)]
        for i in range(8):
            if i == 7 and g0 == nb // 8 - 1:
                break
            lead = cols[g0]
            flip = 1.0 / lead[i][i:i + 1, :]
            pivot = tiles[g0][i:i + 1, :]
            heads = [lead[j][i:i + 1, :] for j in range(8)]
            for g in range(g0, nb // 8):
                if g == g0 and i == 7:
                    continue
                rate = cols[g][i] * flip
                if g == g0:
                    rate = jnp.where(sub > i, rate, 0.0)
                for j in range(i + 1, 8):
                    cols[g][j] = cols[g][j] - rate * heads[j]
                tiles[g] = tiles[g] - rate * pivot
    return jnp.concatenate(tiles, axis=0)


def factor_kernel(gram_ref, sketch_in, current_ref, sketch_ref, r_ref, out_ref,
                  xbuf, parts, obuf, load_sem, store_sem):
    rows, width = current_ref.shape
    pieces = 8
    step = rows // pieces

    def load(c):
        at = pl.ds(c * step, step)
        return pltpu.make_async_copy(current_ref.at[at, :], xbuf.at[at, :], load_sem.at[c])

    def store(c):
        at = pl.ds(c * step, step)
        return pltpu.make_async_copy(obuf.at[at, :], out_ref.at[at, :], store_sem.at[c])

    for c in range(pieces):
        load(c).start()
    for source in range(sketch_ref.shape[0]):
        for m in range(MOST):
            sketch_ref[source, m:m + 1, :] = sketch_in[m, source:source + 1, :]

    n = width
    blocks = n // BLOCK
    hooks = blocks * (BLOCK // 8)
    slab = rows // (hooks - BLOCK // 8)
    state = {"next": 0, "turn": 0}

    def split():
        state["turn"] += 1
        if state["turn"] <= BLOCK // 8 or state["next"] >= rows:
            return
        first = state["next"]
        last = min(rows, first + -(-slab // 16) * 16)
        state["next"] = last
        x = xbuf[first:last, :]
        top = x.astype(BF16)
        parts[first:last, 0:width] = top
        parts[first:last, width:2 * width] = (x - top.astype(F32)).astype(BF16)

    row = lax.broadcasted_iota(jnp.int32, (BLOCK, n), 0)
    col = lax.broadcasted_iota(jnp.int32, (BLOCK, n), 1)
    a = [gram_ref[k * BLOCK:(k + 1) * BLOCK, :] for k in range(blocks)]
    w = [jnp.where(row + k * BLOCK == col, 1.0, 0.0).astype(F32) for k in range(blocks)]
    small_row = lax.broadcasted_iota(jnp.int32, (BLOCK, BLOCK), 0)
    small_col = lax.broadcasted_iota(jnp.int32, (BLOCK, BLOCK), 1)
    unit = jnp.where(small_row == small_col, 1.0, 0.0).astype(F32)
    for k in range(blocks):
        at = slice(k * BLOCK, (k + 1) * BLOCK)
        if k == 1:
            for c in range(pieces):
                load(c).wait()
        both = eliminate(jnp.concatenate([a[k][:, at], unit], axis=1), split)
        diag = jnp.sum(jnp.where(small_row == small_col, both[:, :BLOCK], 0.0), axis=1, keepdims=True)
        scale = 1.0 / jnp.sqrt(diag)
        inv = both[:, BLOCK:] * scale
        r_rows = jnp.dot(inv, a[k], precision=HIGHEST, preferred_element_type=F32)
        lower = {}
        for later in range(k + 1, blocks):
            lower[later] = lax.dot_general(a[later][:, at], inv, (((1,), (1,)), ((), ())),
                                           precision=HIGHEST, preferred_element_type=F32)
            a[later] = a[later] - jnp.dot(lower[later], r_rows, precision=HIGHEST,
                                          preferred_element_type=F32)
        w_rows = jnp.dot(inv, w[k], precision=HIGHEST, preferred_element_type=F32)
        for later in range(k + 1, blocks):
            w[later] = w[later] - jnp.dot(lower[later], w_rows, precision=HIGHEST,
                                          preferred_element_type=F32)
        r_ref[at, :] = jnp.where(row + k * BLOCK <= col, r_rows, 0.0)
        w[k] = w_rows
    inverse = jnp.concatenate(w, axis=0).T
    top = inverse.astype(BF16)
    rest = (inverse - top.astype(F32)).astype(BF16)
    stack = jnp.concatenate([top, top, rest], axis=0)
    for c in range(pieces):
        at = slice(c * step, (c + 1) * step)
        x = parts[at, :]
        x = jnp.concatenate([x, x[:, 0:width]], axis=1)
        obuf[at, :] = jnp.dot(x, stack, preferred_element_type=F32)
        store(c).start()
    for c in range(pieces):
        store(c).wait()


def shards(nh, nl, current, signs, sample_rows, sample_owner):
    rows, width = current.shape
    count = sample_rows.shape[0]
    devices = nh * nl
    total = devices * count
    stages = bits_of(devices)
    vmem = pl.BlockSpec(memory_space=pltpu.VMEM)
    anywhere = pl.BlockSpec(memory_space=pl.ANY)
    dma = pltpu.SemaphoreType.DMA
    chunk = min(256, total // 2)
    gram, picked = pl.pallas_call(
        functools.partial(mix_kernel, nh, nl, count),
        name="mix",
        out_shape=(jax.ShapeDtypeStruct((width, width), F32),
                   jax.ShapeDtypeStruct((MOST, nl, width), F32)),
        in_specs=[anywhere, anywhere, anywhere, anywhere],
        out_specs=(vmem, vmem),
        scratch_shapes=[
            pltpu.VMEM((1, count), jnp.int32),
            pltpu.VMEM((1, count), jnp.int32),
            pltpu.VMEM((rows // LANES, LANES), jnp.int32),
            pltpu.VMEM((1, LANES), F32),
            pltpu.VMEM((rows, width), F32),
            pltpu.VMEM((rows, width), BF16),
            pltpu.VMEM((rows, width), BF16),
            pltpu.VMEM((devices, LANES), F32),
            pltpu.VMEM((chunk, rows), BF16),
            pltpu.VMEM((total, width), F32),
            pltpu.VMEM((total, width), F32),
            pltpu.VMEM((nl, count, width), F32),
            pltpu.VMEM((total, width), F32),
            dma((3,)), dma((8,)), dma((devices,)), dma((devices,)),
            dma((stages,)), dma((stages,)), dma((nl,)), dma((nl,)), dma((nl,)), dma((nl,)),
            dma((stages * nh,)), dma((stages * nh,)),
        ],
        compiler_params=pltpu.CompilerParams(
            collective_id=0, has_side_effects=True, vmem_limit_bytes=VMEM_LIMIT),
    )(sample_rows.reshape(1, count), sample_owner.reshape(1, count), signs.reshape(rows // LANES, LANES), current)
    sketch, r_factor, precond = pl.pallas_call(
        factor_kernel,
        name="factor",
        out_shape=(jax.ShapeDtypeStruct((nl, MOST, width), F32),
                   jax.ShapeDtypeStruct((width, width), F32),
                   jax.ShapeDtypeStruct((rows, width), F32)),
        in_specs=[vmem, vmem, anywhere],
        out_specs=(vmem, vmem, anywhere),
        scratch_shapes=[
            pltpu.VMEM((rows, width), F32),
            pltpu.VMEM((rows, 2 * width), BF16),
            pltpu.VMEM((rows, width), F32),
            dma((8,)), dma((8,)),
        ],
        compiler_params=pltpu.CompilerParams(vmem_limit_bytes=VMEM_LIMIT),
    )(gram, picked, current)
    return (sketch.reshape(1, 1, nl, MOST, width), r_factor, precond)


def solution(mesh):
    placed = (P(("hi", "lo"), None), P(("hi", "lo")), P(("hi", "lo")), P(("hi", "lo"), None))
    return jax.shard_map(
        functools.partial(shards, mesh.shape["hi"], mesh.shape["lo"]),
        mesh=mesh,
        in_specs=placed,
        out_specs=(P("hi", "lo", None, None, None), P(), P(("hi", "lo"), None)),
        check_vma=False,
    )
```
